32 devices in a mesh: dp: 16 (over z, y, x), tensor: 2 (over core).
Axes of the slice: x: 2, y: 2, z: 4, core: 2. Of those that a mesh axis runs over, the one named last changes fastest.
Arguments:
- block_input: bfloat16 [3136, 512], P('dp'), may hold values from -6 to 6
- ln1_gain: float32 [512], replicated, may hold values from 0.1 to 1.9
- ln1_bias: float32 [512], replicated, may hold values from -3 to 3
- w_qkv: bfloat16 [3, 512, 512], P(None, None, 'tensor'), may hold values from -0.25 to 0.25
- qv_bias: float32 [2, 512], P(None, 'tensor'), may hold values from -3 to 3
- bias_table: float32 [169, 16], P(None, 'tensor'), may hold values from -4 to 4
- w_proj: bfloat16 [512, 512], P('tensor'), may hold values from -1 to 1
- proj_bias: float32 [512], replicated, may hold values from -3 to 3
- ln2_gain: float32 [512], replicated, may hold values from 0.1 to 1.9
- ln2_bias: float32 [512], replicated, may hold values from -3 to 3
- w_fc1: bfloat16 [512, 2048], P(None, 'tensor'), may hold values from -0.25 to 0.25
- fc1_bias: float32 [2048], P('tensor'), may hold values from -3 to 3
- w_fc2: bfloat16 [2048, 512], P('tensor'), may hold values from -0.1875 to 0.1875
- fc2_bias: float32 [512], replicated, may hold values from -3 to 3
- region_ids: int32 [4, 49], replicated, may hold values from 0 to 3
- rel_index: int32 [49, 49], replicated, may hold values from 0 to 168
- cotangent: bfloat16 [3136, 512], P('dp'), may hold values from -6 to 6
Outputs:
- block_output: float32 [3136, 512], P('dp')
- dx: float32 [3136, 512], P('dp')
- g_ln1_gain: float32 [512], replicated
- g_ln1_bias: float32 [512], replicated
- g_qkv: float32 [3, 512, 512], P(None, None, 'tensor')
- g_qv_bias: float32 [2, 512], P(None, 'tensor')
- g_table: float32 [169, 16], P(None, 'tensor')
- g_proj: float32 [512, 512], P('tensor')
- g_proj_bias: float32 [512], replicated
- g_ln2_gain: float32 [512], replicated
- g_ln2_bias: float32 [512], replicated
- g_fc1: float32 [512, 2048], P(None, 'tensor')
- g_fc1_bias: float32 [2048], P('tensor')
- g_fc2: float32 [2048, 512], P('tensor')
- g_fc2_bias: float32 [512], replicated
The draws below stay inside these ranges and needn't reach their ends.
All inputs are finite; a program needn't handle non-finite values.
Results may differ from the reference program's by a relative error of at most 0.012.
Values sent between devices are 32-bit elements; how exact they have to be, the bound alone decides.
No kernel may reach another device: no remote copies, remote signals or barrier semaphores. Data moves between devices by JAX's collectives and lax.ppermute only.
A program may use at most 64 MiB of HBM per device.

```python
import jax
import jax.numpy as jnp
from jax import lax

D = 512
HEADS = 16
HID = 2048
IMG_DEV = 1
SIDE = 14
WIN = 7
SHIFT = 3
NWIN = 4
WTOK = 49
TABLE = 169
TOKENS = 3136
N_DP = 16


def set_ends(values, own_key, least, top_value):
    longest = values.shape.index(max(values.shape))
    spots = []
    for shift in (0, 1):
        where = [jax.random.randint(jax.random.fold_in(own_key, axis), (), 0, length) for axis, length in enumerate(values.shape)]
        where[longest] = (where[longest] + shift) % values.shape[longest]
        spots.append(tuple(where))
    return values.at[spots[0]].set(least).at[spots[1]].set(top_value)


def block_scale(rng, extent, pieces, smallest, largest):
    def one(axis_at, shards_of):
        heights = jax.random.uniform(jax.random.fold_in(jax.random.fold_in(rng, 6), axis_at), (shards_of,), jnp.float32, smallest / len(pieces), largest / len(pieces))
        return jnp.repeat(jnp.exp(heights), extent[axis_at] // shards_of).reshape((-1,) + (1,) * (len(extent) - axis_at - 1))

    level = one(*pieces[0])
    for cut in pieces[1:]:
        level = level * one(*cut)
    return level


def scatter_about(rng, extent, scale, limit, cuts=(), kind=jnp.bfloat16):
    values = scale * jax.random.normal(rng, extent, jnp.float32)
    if cuts:
        values = values * block_scale(rng, extent, cuts, -0.22, 0.18)
    return jnp.clip(values, -limit, limit).astype(kind)


def setup_inputs(seed: int = 0) -> dict:
    seeds = jax.random.split(jax.random.key(seed), 18)
    block_input = scatter_about(seeds[0], (TOKENS, D), 1.0, 6.0, ((0, 16),))
    ln1_gain = jnp.clip(1.0 + 0.18 * jax.random.normal(seeds[1], (D,), jnp.float32), 0.1, 1.9)
    ln1_bias = scatter_about(seeds[2], (D,), 0.5, 3.0, (), jnp.float32)
    w_qkv = scatter_about(seeds[3], (3, D, D), D ** -0.5, 0.25, ((2, 2),))
    qv_bias = scatter_about(seeds[4], (2, D), 0.5, 3.0, ((1, 2),), jnp.float32)
    bias_table = scatter_about(seeds[5], (TABLE, HEADS), 1.0, 4.0, ((1, 2),), jnp.float32)
    w_proj = scatter_about(seeds[6], (D, D), (max(D // 16, 1)) ** -0.5, 1.0, ((0, 2),))
    proj_bias = scatter_about(seeds[7], (D,), 0.5, 3.0, (), jnp.float32)
    ln2_gain = jnp.clip(1.0 + 0.18 * jax.random.normal(seeds[8], (D,), jnp.float32), 0.1, 1.9)
    ln2_bias = scatter_about(seeds[9], (D,), 0.5, 3.0, (), jnp.float32)
    w_fc1 = scatter_about(seeds[10], (D, HID), D ** -0.5, 0.25, ((1, 2),))
    fc1_bias = scatter_about(seeds[11], (HID,), 0.5, 3.0, ((0, 2),), jnp.float32)
    w_fc2 = scatter_about(seeds[12], (HID, D), (HID // 2) ** -0.5, 0.1875, ((0, 2),))
    fc2_bias = scatter_about(seeds[13], (D,), 0.5, 3.0, (), jnp.float32)
    region_ids = set_ends(jax.random.randint(seeds[14], (NWIN, WTOK), 0, 4), jax.random.fold_in(seeds[14], 1), 0, 3).astype(jnp.int32)
    rel_index = set_ends(jax.random.randint(seeds[15], (WTOK, WTOK), 0, TABLE), jax.random.fold_in(seeds[15], 1), 0, TABLE - 1).astype(jnp.int32)
    cotangent = scatter_about(seeds[16], (TOKENS, D), 1.0, 6.0, ((0, 16),))
    return dict(block_input=block_input, ln1_gain=ln1_gain, ln1_bias=ln1_bias, w_qkv=w_qkv, qv_bias=qv_bias, bias_table=bias_table, w_proj=w_proj, proj_bias=proj_bias, ln2_gain=ln2_gain, ln2_bias=ln2_bias, w_fc1=w_fc1, fc1_bias=fc1_bias, w_fc2=w_fc2, fc2_bias=fc2_bias, region_ids=region_ids, rel_index=rel_index, cotangent=cotangent)


def layer_stats(values, gain, bias):
    mean = lax.optimization_barrier(jnp.mean(values, -1, keepdims=True))
    centred = values - mean
    var = lax.optimization_barrier(jnp.mean(centred * centred, -1, keepdims=True))
    rstd = lax.rsqrt(var + 1e-05)
    nhat = centred * rstd
    return (nhat * gain + bias, nhat, rstd)

def layer_back(dout, nhat, rstd, gain):
    dnorm = dout * gain
    return rstd * (dnorm - lax.optimization_barrier(jnp.mean(dnorm, -1, keepdims=True)) - nhat * lax.optimization_barrier(jnp.mean(dnorm * nhat, -1, keepdims=True)))

def to_windows(values, nimg):
    width = values.shape[-1]
    per = SIDE // WIN
    grid = values.reshape(nimg, SIDE, SIDE, width)
    grid = jnp.roll(grid, (-SHIFT, -SHIFT), (1, 2))
    grid = grid.reshape(nimg, per, WIN, per, WIN, width).transpose(0, 1, 3, 2, 4, 5)
    return grid.reshape(-1, width)

def from_windows(values, nimg):
    width = values.shape[-1]
    per = SIDE // WIN
    grid = values.reshape(nimg, per, per, WIN, WIN, width).transpose(0, 1, 3, 2, 4, 5)
    grid = grid.reshape(nimg, SIDE, SIDE, width)
    grid = jnp.roll(grid, (SHIFT, SHIFT), (1, 2))
    return grid.reshape(-1, width)

def gelu_value(u):
    return 0.5 * u * (1.0 + lax.erf(u * 0.7071067811865476))

def gelu_slope(u):
    return 0.5 * (1.0 + lax.erf(u * 0.7071067811865476)) + u * jnp.exp(-0.5 * u * u) * 0.3989422804014327

def inner(left, right):
    return lax.dot_general(left, right, (((0,), (0,)), ((), ())), preferred_element_type=jnp.float32)

def outer(left, right):
    return lax.dot_general(left, right, (((1,), (1,)), ((), ())), preferred_element_type=jnp.float32)

def mixed(form, left, right):
    return jnp.einsum(form, left.astype(jnp.float32), right.astype(jnp.float32), precision=lax.Precision.HIGHEST)

def block_pass(x, gvals, ln1_gain, ln1_bias, w_qkv, qv_bias, w_proj, proj_bias, ln2_gain, ln2_bias, w_fc1, fc1_bias, w_fc2, fc2_bias, bias, mask):
    nimg = x.shape[0] // (SIDE * SIDE)
    heads = bias.shape[0]
    hdim = w_qkv.shape[2] // heads
    scale = hdim ** (-0.5)
    shape5 = (nimg, NWIN, WTOK, heads, hdim)
    xf = x.astype(jnp.float32)
    anorm, nhat1, rstd1 = layer_stats(xf, ln1_gain, ln1_bias)
    aw = to_windows(anorm.astype(jnp.bfloat16), nimg)
    query = ((jnp.dot(aw, w_qkv[0], preferred_element_type=jnp.float32) + qv_bias[0]) * scale).astype(jnp.bfloat16)
    keys = jnp.dot(aw, w_qkv[1], preferred_element_type=jnp.float32).astype(jnp.bfloat16)
    values = (jnp.dot(aw, w_qkv[2], preferred_element_type=jnp.float32) + qv_bias[1]).astype(jnp.bfloat16)
    q5 = query.reshape(shape5)
    k5 = keys.reshape(shape5)
    v5 = values.reshape(shape5)
    scores = mixed('nwihd,nwjhd->nwhij', q5, k5) + bias[None, None] + mask[None, :, None]
    expo = jnp.exp(scores)
    total = lax.optimization_barrier(jnp.sum(expo, -1, keepdims=True))
    probs = expo / total
    lse = jnp.log(total)
    attn5 = mixed('nwhij,nwjhd->nwihd', probs.astype(jnp.bfloat16), v5).astype(jnp.bfloat16)
    attn_flat = attn5.reshape(-1, heads * hdim)
    hres = xf + from_windows(jnp.dot(attn_flat, w_proj, preferred_element_type=jnp.float32), nimg) + proj_bias
    cnorm, nhat2, rstd2 = layer_stats(hres, ln2_gain, ln2_bias)
    cb = cnorm.astype(jnp.bfloat16)
    upre = jnp.dot(cb, w_fc1, preferred_element_type=jnp.float32) + fc1_bias
    zact = gelu_value(upre).astype(jnp.bfloat16)
    y = hres + jnp.dot(zact, w_fc2, preferred_element_type=jnp.float32) + fc2_bias
    gf = gvals.astype(jnp.float32)
    g_fc2_bias = lax.optimization_barrier(jnp.sum(gf, 0))
    g_fc2 = inner(zact, gvals)
    du = outer(gvals, w_fc2) * gelu_slope(upre)
    g_fc1_bias = lax.optimization_barrier(jnp.sum(du, 0))
    dub = du.astype(jnp.bfloat16)
    g_fc1 = inner(cb, dub)
    dcn = outer(dub, w_fc1)
    g_ln2_gain = lax.optimization_barrier(jnp.sum(dcn * nhat2, 0))
    g_ln2_bias = lax.optimization_barrier(jnp.sum(dcn, 0))
    dh = gf + layer_back(dcn, nhat2, rstd2, ln2_gain)
    g_proj_bias = lax.optimization_barrier(jnp.sum(dh, 0))
    dhw = to_windows(dh, nimg).astype(jnp.bfloat16)
    g_proj = inner(attn_flat, dhw)
    dout = outer(dhw, w_proj).astype(jnp.bfloat16)
    d5 = dout.reshape(shape5)
    scores = mixed('nwihd,nwjhd->nwhij', q5, k5) + bias[None, None] + mask[None, :, None]
    probs = jnp.exp(scores - lse)
    pb = probs.astype(jnp.bfloat16)
    dprob = mixed('nwihd,nwjhd->nwhij', d5, v5)
    delta = lax.optimization_barrier(jnp.sum(d5.astype(jnp.float32) * attn5.astype(jnp.float32), -1)).transpose(0, 1, 3, 2)[..., None]
    dscore = probs * (dprob - delta)
    dv = mixed('nwhij,nwihd->nwjhd', pb, d5).reshape(-1, heads * hdim)
    dbias = lax.optimization_barrier(jnp.sum(dscore, (0, 1)))
    dsb = dscore.astype(jnp.bfloat16)
    dq = (mixed('nwhij,nwjhd->nwihd', dsb, k5) * scale).reshape(-1, heads * hdim)
    dk = mixed('nwhij,nwihd->nwjhd', dsb, q5).reshape(-1, heads * hdim)
    g_qv_bias = jnp.stack([lax.optimization_barrier(jnp.sum(dq, 0)), lax.optimization_barrier(jnp.sum(dv, 0))])
    dqb = dq.astype(jnp.bfloat16)
    dkb = dk.astype(jnp.bfloat16)
    dvb = dv.astype(jnp.bfloat16)
    g_qkv = jnp.stack([inner(aw, dqb), inner(aw, dkb), inner(aw, dvb)])
    daw = outer(dqb, w_qkv[0]) + outer(dkb, w_qkv[1]) + outer(dvb, w_qkv[2])
    dan = from_windows(daw, nimg)
    g_ln1_gain = lax.optimization_barrier(jnp.sum(dan * nhat1, 0))
    g_ln1_bias = lax.optimization_barrier(jnp.sum(dan, 0))
    dx = dh + layer_back(dan, nhat1, rstd1, ln1_gain)
    grads = (g_ln1_gain, g_ln1_bias, g_qkv, g_qv_bias, dbias, g_proj, g_proj_bias, g_ln2_gain, g_ln2_bias, g_fc1, g_fc1_bias, g_fc2, g_fc2_bias)
    return (y, dx, grads)

def reference(block_input, ln1_gain, ln1_bias, w_qkv, qv_bias, bias_table, w_proj, proj_bias, ln2_gain, ln2_bias, w_fc1, fc1_bias, w_fc2, fc2_bias, region_ids, rel_index, cotangent):
    onehot = (rel_index.reshape(-1)[:, None] == lax.iota(jnp.int32, TABLE)[None, :]).astype(jnp.float32)
    bias = jnp.dot(onehot, bias_table, precision=lax.Precision.HIGHEST).T.reshape(HEADS, WTOK, WTOK)
    same = region_ids[:, :, None] == region_ids[:, None, :]
    mask = jnp.where(same, jnp.float32(0.0), jnp.float32(-100.0))
    group = IMG_DEV * SIDE * SIDE
    xs = block_input.reshape(N_DP, group, D)
    gs = cotangent.reshape(N_DP, group, D)
    init = (jnp.zeros((D,), jnp.float32), jnp.zeros((D,), jnp.float32), jnp.zeros((3, D, D), jnp.float32), jnp.zeros((2, D), jnp.float32), jnp.zeros((HEADS, WTOK, WTOK), jnp.float32), jnp.zeros((D, D), jnp.float32), jnp.zeros((D,), jnp.float32), jnp.zeros((D,), jnp.float32), jnp.zeros((D,), jnp.float32), jnp.zeros((D, HID), jnp.float32), jnp.zeros((HID,), jnp.float32), jnp.zeros((HID, D), jnp.float32), jnp.zeros((D,), jnp.float32))

    def advance(carry, item):
        xb, gb = item
        yb, dxb, grads = block_pass(xb, gb, ln1_gain, ln1_bias, w_qkv, qv_bias, w_proj, proj_bias, ln2_gain, ln2_bias, w_fc1, fc1_bias, w_fc2, fc2_bias, bias, mask)
        return (tuple((c + d for c, d in zip(carry, grads))), (yb, dxb))
    sums, (ys, dxs) = lax.scan(advance, init, (xs, gs))
    dbias = sums[4].reshape(HEADS, WTOK * WTOK)
    g_table = lax.dot_general(onehot, dbias, (((0,), (1,)), ((), ())), precision=lax.Precision.HIGHEST)
    return (ys.reshape(-1, D), dxs.reshape(-1, D), sums[0], sums[1], sums[2], sums[3], g_table, sums[5], sums[6], sums[7], sums[8], sums[9], sums[10], sums[11], sums[12])
```

```python
import functools

import jax
import jax.numpy as jnp
import numpy as np
from jax import lax
from jax.experimental import pallas as pl
from jax.experimental.pallas import tpu as pltpu
from jax.sharding import PartitionSpec as P

SIDE = 14
WIN = 7
SHIFT = 3
NWIN = 4
WTOK = 49
WPAD = 64
TABLE = 169
BLOCKS = 16
F32 = jnp.float32
BF16 = jnp.bfloat16

ORDERS = ((2, 4, 1, 8), (4, 1, 8, 2), (1, 2, 4, 8))


def dot(left, right, dims=((1,), (0,))):
    return lax.dot_general(left, right, (dims, ((), ())), preferred_element_type=F32)


NT = ((1,), (1,))
TN = ((0,), (0,))


def window_rows(nimg):
    per = SIDE // WIN
    rows = np.zeros((nimg * NWIN * WPAD, nimg * SIDE * SIDE), np.float32)
    for img in range(nimg):
        for win in range(NWIN):
            for pos in range(WTOK):
                r = (win // per) * WIN + pos // WIN
                c = (win % per) * WIN + pos % WIN
                src = ((r + SHIFT) % SIDE) * SIDE + (c + SHIFT) % SIDE
                rows[(img * NWIN + win) * WPAD + pos, img * SIDE * SIDE + src] = 1.0
    return rows


def stats(values):
    mean = jnp.mean(values, -1, keepdims=True)
    centred = values - mean
    var = jnp.mean(centred * centred, -1, keepdims=True)
    rstd = lax.rsqrt(var + 1e-05)
    return centred * rstd, rstd


def norm_back(dout, nhat, rstd, gain):
    dnorm = dout * gain
    return rstd * (
        dnorm
        - jnp.mean(dnorm, -1, keepdims=True)
        - nhat * jnp.mean(dnorm * nhat, -1, keepdims=True)
    )


def head_mask(heads, width):
    hdim = width // heads
    row = lax.broadcasted_iota(jnp.int32, (heads * WPAD, width), 0) // WPAD
    col = lax.broadcasted_iota(jnp.int32, (heads * WPAD, width), 1) // hdim
    return jnp.where(row == col, 1.0, 0.0).astype(F32)


def position_bias(table_ref, rel_ref, tab_s, idx_s, bias_s, heads):
    tab_s[...] = jnp.zeros_like(tab_s)
    tab_s[0:TABLE, 0:heads] = table_ref[...]
    idx_s[...] = jnp.zeros_like(idx_s)
    idx_s[0:WTOK, 0:WTOK] = rel_ref[...]
    flipped = tab_s[...].T
    idx = idx_s[...]
    low = idx & 127
    first = idx < 128
    pad = lax.broadcasted_iota(jnp.int32, (WPAD, WPAD), 1) >= WTOK
    for h in range(heads):
        a = jnp.take_along_axis(jnp.broadcast_to(flipped[h : h + 1, 0:128], (WPAD, 128)), low, axis=1)
        b = jnp.take_along_axis(jnp.broadcast_to(flipped[h : h + 1, 128:256], (WPAD, 128)), low, axis=1)
        got = jnp.where(first, a, b)[:, 0:WPAD]
        bias_s[h * WPAD : (h + 1) * WPAD, :] = jnp.where(pad, -1e30, got)


def region_mask(rid_ref, rid_s):
    rid_s[...] = jnp.zeros_like(rid_s)
    rid_s[0:NWIN, 0:WTOK] = rid_ref[...].astype(F32)
    rows = rid_s[...]
    cols = rows.T
    out = []
    for w in range(NWIN):
        same = cols[0:WPAD, w : w + 1] == rows[w : w + 1, 0:WPAD]
        out.append(jnp.where(same, 0.0, -100.0).astype(F32))
    return out


def by_head(values, mask, heads):
    return jnp.concatenate([values] * heads, 0) * mask


def over_heads(values, mask, heads):
    kept = values * mask
    total = kept[0:WPAD]
    for h in range(1, heads):
        total = total + kept[h * WPAD : (h + 1) * WPAD]
    return total


def probabilities(qb, kw, bias, mask, heads):
    s = dot(qb, kw, NT) + bias + jnp.concatenate([mask] * heads, 0)
    e = jnp.exp(s)
    return e / jnp.sum(e, -1, keepdims=True)


def attend_kernel(
    x_ref, gain_ref, shift_ref, wqkv_ref, qvb_ref, table_ref, rel_ref, rid_ref, wproj_ref, pw_ref, pwt_ref,
    part_ref, q_ref, k_ref, v_ref, o_ref,
    tab_s, idx_s, bias_s, rid_s, ow_s, hm_s,
):
    heads = table_ref.shape[1]
    width = wqkv_ref.shape[2]
    scale = (width // heads) ** (-0.5)
    nhat, _ = stats(x_ref[...].astype(F32))
    a = (nhat * gain_ref[...] + shift_ref[...]).astype(BF16)
    pw = pw_ref[...]
    q = ((dot(a, wqkv_ref[0]) + qvb_ref[0:1, :]) * scale).astype(BF16)
    q_ref[...] = dot(pw, q).astype(BF16)
    k = dot(a, wqkv_ref[1]).astype(BF16)
    k_ref[...] = dot(pw, k).astype(BF16)
    v = (dot(a, wqkv_ref[2]) + qvb_ref[1:2, :]).astype(BF16)
    v_ref[...] = dot(pw, v).astype(BF16)
    position_bias(table_ref, rel_ref, tab_s, idx_s, bias_s, heads)
    masks = region_mask(rid_ref, rid_s)
    hm_s[...] = head_mask(heads, width)
    bias = bias_s[...]
    hm = hm_s[...]
    hmb = hm.astype(BF16)
    for w in range(q_ref.shape[0] // WPAD):
        rows = slice(w * WPAD, (w + 1) * WPAD)
        qb = by_head(q_ref[rows, :], hmb, heads)
        p = probabilities(qb, k_ref[rows, :], bias, masks[w % NWIN], heads)
        full = dot(p.astype(BF16), v_ref[rows, :])
        ow_s[rows, :] = over_heads(full, hm, heads).astype(BF16)
    o = dot(pwt_ref[...], ow_s[...]).astype(BF16)
    o_ref[...] = o
    part_ref[...] = dot(o, wproj_ref[...])


def mlp_kernel(
    me_ref, x_ref, own_ref, other_ref, pbias_ref, gain_ref, shift_ref, w1_ref, b1_ref, w2_ref, cot_ref,
    h_ref, mlp_ref, dc_ref, small_ref, s0lo, s0hi, s1lo, s1hi, s2lo, s2hi,
    g1_s, g2_s,
):
    hid = w1_ref.shape[1]
    dim = w1_ref.shape[0]
    h = x_ref[...].astype(F32) + own_ref[...] + other_ref[...] + pbias_ref[...]
    h_ref[...] = h
    nhat, _ = stats(h)
    c = (nhat * gain_ref[...] + shift_ref[...]).astype(BF16)
    cot = cot_ref[...]
    small_ref[0:1, :] = jnp.sum(cot.astype(F32), 0, keepdims=True)
    step = 256
    mlp = jnp.zeros(h.shape, F32)
    dc = jnp.zeros(h.shape, F32)
    for j in range(hid // step):
        cols = slice(j * step, (j + 1) * step)
        w1 = w1_ref[:, cols]
        w2 = w2_ref[cols, :]
        u = dot(c, w1) + b1_ref[:, cols]
        cdf = 0.5 * (1.0 + lax.erf(u * 0.7071067811865476))
        z = (u * cdf).astype(BF16)
        slope = cdf + u * jnp.exp(-0.5 * u * u) * 0.3989422804014327
        du = dot(cot, w2, NT) * slope
        at = (j * step) % dim
        small_ref[1 + (j * step) // dim : 2 + (j * step) // dim, at : at + step] = jnp.sum(du, 0, keepdims=True)
        dub = du.astype(BF16)
        g2_s[cols, :] = dot(z, cot, TN)
        g1_s[:, cols] = dot(c, dub, TN)
        mlp = mlp + dot(z, w2)
        dc = dc + dot(dub, w1, NT)
    mlp_ref[...] = mlp
    dc_ref[...] = dc
    fill_streams(me_ref[0], STREAMS_A, ((s0lo, s0hi), (s1lo, s1hi), (s2lo, s2hi)), (g1_s, g2_s))


def tail_kernel(
    me_ref, own_ref, other_ref, mown_ref, mother_ref, fbias_ref, h_ref, x_ref, cot_ref, gain2_ref, gain1_ref, shift1_ref,
    wqkv_ref, wproj_ref, q_ref, k_ref, v_ref, o_ref, table_ref, rel_ref, rid_ref, pw_ref, pwt_ref,
    out_ref, dh_ref, da_ref, small_ref, dbias_ref, s0lo, s0hi, s1lo, s1hi, s2lo, s2hi,
    tab_s, idx_s, bias_s, rid_s, hm_s, dq_s, dk_s, dv_s, gq_s, gp_s,
):
    heads = table_ref.shape[1]
    width = wqkv_ref.shape[2]
    scale = (width // heads) ** (-0.5)
    h = h_ref[...]
    out_ref[...] = h + mown_ref[...] + mother_ref[...] + fbias_ref[...]
    dc = own_ref[...] + other_ref[...]
    nhat2, rstd2 = stats(h)
    dh = cot_ref[...].astype(F32) + norm_back(dc, nhat2, rstd2, gain2_ref[...])
    dh_ref[...] = dh
    small_ref[0:1, :] = jnp.sum(dh, 0, keepdims=True)
    small_ref[1:2, :] = jnp.sum(dc * nhat2, 0, keepdims=True)
    small_ref[2:3, :] = jnp.sum(dc, 0, keepdims=True)
    dhb = dh.astype(BF16)
    gp_s[...] = dot(o_ref[...], dhb, TN)
    do = dot(dhb, wproj_ref[...], NT).astype(BF16)
    dow = dot(pw_ref[...], do).astype(BF16)
    position_bias(table_ref, rel_ref, tab_s, idx_s, bias_s, heads)
    masks = region_mask(rid_ref, rid_s)
    hm_s[...] = head_mask(heads, width)
    bias = bias_s[...]
    hm = hm_s[...]
    hmb = hm.astype(BF16)
    dbias = jnp.zeros(bias.shape, F32)
    sum_q = jnp.zeros((1, width), F32)
    sum_v = jnp.zeros((1, width), F32)
    for w in range(q_ref.shape[0] // WPAD):
        rows = slice(w * WPAD, (w + 1) * WPAD)
        kw = k_ref[rows, :]
        qb = by_head(q_ref[rows, :], hmb, heads)
        p = probabilities(qb, kw, bias, masks[w % NWIN], heads)
        db = by_head(dow[rows, :], hmb, heads)
        dp = dot(db, v_ref[rows, :], NT)
        ds = p * (dp - jnp.sum(p * dp, -1, keepdims=True))
        dbias = dbias + ds
        dv = dot(p.astype(BF16), db, TN)
        dsb = ds.astype(BF16)
        dq = over_heads(dot(dsb, kw), hm, heads) * scale
        dk = dot(dsb, qb, TN)
        sum_q = sum_q + jnp.sum(dq, 0, keepdims=True)
        sum_v = sum_v + jnp.sum(dv, 0, keepdims=True)
        dq_s[rows, :] = dq.astype(BF16)
        dk_s[rows, :] = dk.astype(BF16)
        dv_s[rows, :] = dv.astype(BF16)
    dbias_ref[...] = dbias
    small_ref[3:4, 0:width] = sum_q
    small_ref[3:4, width : 2 * width] = sum_v
    nhat1, _ = stats(x_ref[...].astype(F32))
    a = (nhat1 * gain1_ref[...] + shift1_ref[...]).astype(BF16)
    pwt = pwt_ref[...]
    da = jnp.zeros(h.shape, F32)
    for m, ref in enumerate((dq_s, dk_s, dv_s)):
        d = dot(pwt, ref[...]).astype(BF16)
        gq_s[m] = dot(a, d, TN)
        da = da + dot(d, wqkv_ref[m], NT)
    da_ref[...] = da
    fill_streams(
        me_ref[0], STREAMS_B, ((s0lo, s0hi), (s1lo, s1hi), (s2lo, s2hi)), (gq_s.at[0], gq_s.at[1], gq_s.at[2], gp_s)
    )


def first_kernel(own_ref, other_ref, x_ref, dh_ref, gain_ref, dx_ref, small_ref):
    da = own_ref[...] + other_ref[...]
    nhat, rstd = stats(x_ref[...].astype(F32))
    small_ref[0:1, :] = jnp.sum(da * nhat, 0, keepdims=True)
    small_ref[1:2, :] = jnp.sum(da, 0, keepdims=True)
    dx_ref[...] = dh_ref[...] + norm_back(da, nhat, rstd, gain_ref[...])


STREAMS_A = (
    tuple((0, 32, t) for t in range(0, 5)),
    tuple((0, 32, t) for t in range(5, 8)) + ((1, 64, 0),),
    tuple((1, 64, t) for t in range(1, 4)),
)
STREAMS_B = (
    ((0, 32, 0), (0, 32, 1), (3, 16, 0), (3, 16, 1)),
    ((2, 32, 0), (2, 32, 1)),
    ((1, 32, 0), (1, 32, 1), (3, 16, 2), (3, 16, 3)),
)


def block_at(me, order, place):
    flips = sum(bit for i, bit in enumerate(order) if place & (8 >> i))
    return lax.bitwise_xor(me, jnp.int32(flips))


def stream_rows(stream):
    return sum(rows for _, rows, _ in stream)


def fill_streams(me, streams, halves, grads):
    for stream, (lo, hi), order in zip(streams, halves, ORDERS):
        for place in range(BLOCKS):
            block = block_at(me, order, place)
            half = lo if place < BLOCKS // 2 else hi
            at = 0
            for g, rows, tile in stream:
                src = pl.ds(pl.multiple_of(block * rows, rows), rows)
                half[place % (BLOCKS // 2), at : at + rows, :] = grads[g][src, tile * 128 : (tile + 1) * 128]
                at += rows


def collect_kernel(streams, npieces, me_ref, *refs):
    pieces = refs[: len(streams) * npieces]
    outs = refs[len(streams) * npieces :]
    me = me_ref[0]
    for s, (stream, order) in enumerate(zip(streams, ORDERS)):
        mine = pieces[s * npieces : (s + 1) * npieces]
        places = [(ref, i) for ref in mine for i in range(ref.shape[0])]
        for place, (ref, i) in enumerate(places):
            block = block_at(me, order, place)
            at = 0
            for g, rows, tile in stream:
                dst = pl.ds(pl.multiple_of(block * rows, rows), rows)
                outs[g][dst, tile * 128 : (tile + 1) * 128] = ref[i, at : at + rows, :]
                at += rows


def vmem(n):
    return [pl.BlockSpec(memory_space=pltpu.VMEM) for _ in range(n)]


def smem():
    return pl.BlockSpec(memory_space=pltpu.SMEM)


def call(kernel, outs, args, scratch=(), scalars=0, name=None):
    return pl.pallas_call(
        kernel,
        out_shape=tuple(jax.ShapeDtypeStruct(s, d) for s, d in outs),
        in_specs=[smem() for _ in range(scalars)] + vmem(len(args) - scalars),
        out_specs=tuple(vmem(len(outs))),
        scratch_shapes=[pltpu.VMEM(s, d) for s, d in scratch],
        name=name,
    )(*args)


def swap(values, bit, size):
    return lax.ppermute(values, "dp", [(i, i ^ bit) for i in range(size)])


def partner(values):
    return lax.ppermute(values, "tensor", [(0, 1), (1, 0)])


def reduce_streams(halves, size):
    keep = [lo for lo, _ in halves]
    send = [hi for _, hi in halves]
    for r in range(4):
        got = [swap(s, o[r], size) for s, o in zip(send, ORDERS)]
        h = 8 >> (r + 1)
        if r < 3:
            send = [k[h:] + g[h:] for k, g in zip(keep, got)]
            keep = [k[:h] + g[:h] for k, g in zip(keep, got)]
        else:
            keep = [k + g for k, g in zip(keep, got)]
    bit = BLOCKS
    while bit < size:
        keep = [k + swap(k, bit, size) for k in keep]
        bit *= 2
    pieces = [[k] for k in keep]
    for r in range(3, -1, -1):
        got = [swap(k, o[r], size) for k, o in zip(keep, ORDERS)]
        for p, g in zip(pieces, got):
            p.append(g)
        if r:
            keep = [jnp.concatenate([k, g], 0) for k, g in zip(keep, got)]
    return pieces


def collect(streams, pieces, me, outs, name):
    flat = [p for piece in pieces for p in piece]
    kernel = functools.partial(collect_kernel, streams, len(pieces[0]))
    return call(kernel, outs, [me] + flat, scalars=1, name=name)


def body(
    size,
    block_input,
    ln1_gain,
    ln1_bias,
    w_qkv,
    qv_bias,
    bias_table,
    w_proj,
    proj_bias,
    ln2_gain,
    ln2_bias,
    w_fc1,
    fc1_bias,
    w_fc2,
    fc2_bias,
    region_ids,
    rel_index,
    cotangent,
):
    tokens, dim = block_input.shape
    nimg = tokens // (SIDE * SIDE)
    heads = bias_table.shape[1]
    width = w_qkv.shape[2]
    hid = w_fc1.shape[1]
    wrows = nimg * NWIN * WPAD
    rows_np = window_rows(nimg)
    pw = jnp.asarray(rows_np, BF16)
    pwt = jnp.asarray(rows_np.T, BF16)
    me = lax.bitwise_and(lax.axis_index("dp"), BLOCKS - 1).astype(jnp.int32).reshape(1)
    row = lambda v: v.reshape(1, -1)
    g1, b1, g2, b2 = row(ln1_gain), row(ln1_bias), row(ln2_gain), row(ln2_bias)
    att_scratch = [((256, 128), F32), ((WPAD, 128), jnp.int32), ((heads * WPAD, WPAD), F32), ((128, 128), F32)]
    tok = ((tokens, dim), F32)
    win = ((wrows, width), BF16)

    part, qw, kw, vw, otok = call(
        attend_kernel,
        [tok, win, win, win, ((tokens, width), BF16)],
        [block_input, g1, b1, w_qkv, qv_bias, bias_table, rel_index, region_ids, w_proj, pw, pwt],
        att_scratch + [win, ((heads * WPAD, width), F32)],
        name="attend",
    )
    other = partner(part)

    def halves(streams):
        return [((BLOCKS // 2, stream_rows(s), 128), F32) for s in streams for _ in range(2)]

    h, mlp, dc, small2, *sa = call(
        mlp_kernel,
        [tok, tok, tok, ((1 + hid // dim, dim), F32)] + halves(STREAMS_A),
        [me, block_input, part, other, row(proj_bias), g2, b2, w_fc1, row(fc1_bias), w_fc2, cotangent],
        [((dim, hid), F32), ((hid, dim), F32)],
        scalars=1,
        name="mlp",
    )
    dc_other = partner(dc)
    mlp_other = partner(mlp)
    pieces_a = reduce_streams(list(zip(sa[0::2], sa[1::2])), size)

    out, dh, da, small3, dbias, *sb = call(
        tail_kernel,
        [tok, tok, tok, ((4, dim), F32), ((heads * WPAD, WPAD), F32)] + halves(STREAMS_B),
        [me, dc, dc_other, mlp, mlp_other, row(fc2_bias), h, block_input, cotangent, g2, g1, b1]
        + [w_qkv, w_proj, qw, kw, vw, otok, bias_table, rel_index, region_ids, pw, pwt],
        att_scratch + [((heads * WPAD, width), F32), win, win, win, ((3, dim, width), F32), ((width, dim), F32)],
        scalars=1,
        name="tail",
    )
    da_other = partner(da)
    pieces_b = reduce_streams(list(zip(sb[0::2], sb[1::2])), size)
    dx, small4 = call(first_kernel, [tok, ((2, dim), F32)], [da, da_other, block_input, dh, g1], name="first")

    onehot = (rel_index.reshape(-1)[:, None] == lax.iota(jnp.int32, TABLE)[None, :]).astype(F32)
    flat = dbias.reshape(heads, WPAD, WPAD)[:, :WTOK, :WTOK].reshape(heads, WTOK * WTOK)
    g_table = lax.dot_general(onehot, flat, (((0,), (1,)), ((), ())), precision=lax.Precision.HIGHEST)
    nt = -(-TABLE * heads // dim)
    table_rows = jnp.pad(g_table.reshape(-1), (0, nt * dim - TABLE * heads)).reshape(nt, dim)
    small = jnp.concatenate([small2, small3, small4, table_rows], 0)
    bit = 1
    while bit < size:
        small = small + swap(small, bit, size)
        bit *= 2

    g_fc1, g_fc2 = collect(STREAMS_A, pieces_a, me, [((dim, hid), F32), ((hid, dim), F32)], "collect_mlp")
    gq, gk, gv, g_proj = collect(
        STREAMS_B, pieces_b, me, [((dim, width), F32)] * 3 + [((width, dim), F32)], "collect_att"
    )
    g_qkv = jnp.stack([gq, gk, gv])
    n2 = 1 + hid // dim
    return (
        out,
        dx,
        small[n2 + 4],
        small[n2 + 5],
        g_qkv,
        small[n2 + 3].reshape(2, width),
        small[n2 + 6 :].reshape(-1)[: TABLE * heads].reshape(TABLE, heads),
        g_proj,
        small[n2],
        small[n2 + 1],
        small[n2 + 2],
        g_fc1,
        small[1:n2].reshape(-1),
        g_fc2,
        small[0],
    )


def solution(mesh):
    return jax.shard_map(
        functools.partial(body, mesh.shape["dp"]),
        mesh=mesh,
        in_specs=(
            P("dp", None),
            P(),
            P(),
            P(None, None, "tensor"),
            P(None, "tensor"),
            P(None, "tensor"),
            P("tensor", None),
            P(),
            P(),
            P(),
            P(None, "tensor"),
            P("tensor"),
            P("tensor", None),
            P(),
            P(),
            P(),
            P("dp", None),
        ),
        out_specs=(
            P("dp", None),
            P("dp", None),
            P(),
            P(),
            P(None, None, "tensor"),
            P(None, "tensor"),
            P(None, "tensor"),
            P("tensor", None),
            P(),
            P(),
            P(),
            P(None, "tensor"),
            P("tensor"),
            P("tensor", None),
            P(),
        ),
        check_vma=False,
    )
```
